32 devices in a mesh: groups: 2 (over y), rows: 16 (over z, x, core).
Axes of the slice: x: 2, y: 2, z: 4, core: 2. Of those that a mesh axis runs over, the one named last changes fastest.
Arguments:
- documents: bfloat16 [16384, 8192], P(('groups', 'rows')), parts along dimension 0, may hold values from -6 to 6
- kernel_inverse: bfloat16 [8192, 8192], P(None, 'rows'), as said below
- queries: bfloat16 [8192, 256], P('rows'), may hold values from -0.0625 to 0.0625
Outputs:
- scores: float32 [16384, 256], P(('groups', 'rows')), parts along dimension 0
The draws below stay inside these ranges and needn't reach their ends.
There are 2 independent parts, one for each index of `groups`. The reference program is written for one: setup_inputs(seed, part) draws one part's arguments, and reference() takes and returns one part's arrays. A program takes and returns all parts, laid end to end along the dimension named above; an argument that names none is the same for every part. Nothing has to cross between parts.
Inputs may be any that keep to these rules, and one draw needn't show every extreme that they name: kernel_inverse is exactly symmetric.
All inputs are finite; a program needn't handle non-finite values.
Results may differ from the reference program's by a relative error of at most 0.0029.
Values may be sent and summed in bfloat16 or wider, within the bound.
A program may use at most 64 MiB of HBM per device.

```python
import math
import jax
import jax.numpy as jnp
from jax import lax

K = 8192
M = 256
DOCS = 8192


def draw_kernel_inverse(key, part):
    key_off = jax.random.fold_in(key, 11)
    key_diag = jax.random.fold_in(key, 12)
    raw = jax.random.normal(key_off, (K, K), jnp.float32)
    diag = jax.random.uniform(key_diag, (K,), jnp.float32, 0.8, 2.0)
    scaled = raw * (0.3 / math.sqrt(K))
    sym = (scaled + scaled.T) * 0.70710678
    rows_id = lax.broadcasted_iota(jnp.int32, (K, K), 0)
    cols_id = lax.broadcasted_iota(jnp.int32, (K, K), 1)
    full = jnp.where(rows_id == cols_id, diag[:, None], sym)
    return full.astype(jnp.bfloat16)


def levels(stream_key, extent, split, smallest, largest):
    def one(axis_at, shards_of):
        steps = jax.random.uniform(jax.random.fold_in(jax.random.fold_in(stream_key, 6), axis_at), (shards_of,), jnp.float32, smallest / len(split), largest / len(split))
        return jnp.repeat(jnp.exp(steps), extent[axis_at] // shards_of).reshape((-1,) + (1,) * (len(extent) - axis_at - 1))

    gain = one(*split[0])
    for cut in split[1:]:
        gain = gain * one(*cut)
    return gain


def bell_draw(own_key, dims, deviation, most, split=(), held_as=jnp.bfloat16):
    level = levels(own_key, dims, split, -0.22, 0.18) if split else 1.0
    array = jax.random.normal(own_key, dims, jnp.float32) * deviation * level
    return jnp.minimum(jnp.maximum(array, -most), most).astype(held_as)


def setup_inputs(seed: int = 0, part: int = 0) -> dict:
    arg_keys = jax.random.split(jax.random.key(seed), 4)
    part_keys = jax.random.split(jax.random.fold_in(arg_keys[3], part), 4)
    return {
        "documents": bell_draw(part_keys[0], (DOCS, K), 1.0, 6.0, ((0, 16),)),
        "kernel_inverse": draw_kernel_inverse(jax.random.fold_in(arg_keys[3], 71), part),
        "queries": bell_draw(arg_keys[2], (K, M), K ** -0.5, 0.0625, ((0, 16),)),
    }


def reference(documents, kernel_inverse, queries):
    precond = jnp.dot(kernel_inverse.astype(jnp.float32), queries.astype(jnp.float32), preferred_element_type=jnp.float32).astype(jnp.bfloat16)
    return jnp.dot(documents.astype(jnp.float32), precond.astype(jnp.float32), preferred_element_type=jnp.float32)
```

```python
import functools
import math

import jax
import jax.numpy as jnp
from jax import lax
from jax.experimental import pallas as pl
from jax.experimental.pallas import tpu as pltpu
from jax.sharding import PartitionSpec as P

MESH = pl.DeviceIdType.MESH
PIECES = 4


def plain(documents, kernel_inverse, queries):
    whole_queries = lax.all_gather(queries, "rows", axis=0, tiled=True)
    own_rows = lax.dot_general(
        kernel_inverse, whole_queries, (((0,), (0,)), ((), ())), preferred_element_type=jnp.float32
    ).astype(jnp.bfloat16)
    return jnp.dot(
        documents,
        lax.all_gather(own_rows, "rows", axis=0, tiled=True),
        preferred_element_type=jnp.float32,
    )


def kernel(
    n, X, docs_hbm, kinv_hbm, q_hbm, out_ref,
    docs, kinv, qbuf, pbuf, acct,
    load_sem, q_recv, q_ring, q_sib, p_recv, p_ring, p_sib, p_y,
):
    g, me = lax.axis_index("groups"), lax.axis_index("rows")
    og = 1 - g
    R = n // 2
    Z = R // X
    H = R // 2
    half, width = qbuf.shape[2], qbuf.shape[3]
    depth = 2 * half
    c = lax.rem(me, 2)
    chip = lax.div(me, 2)
    z, x = lax.div(chip, X), lax.rem(chip, X)
    first = lax.div(Z - z, Z)
    odd = lax.rem(x, 2)
    k = first * (X * (Z - 1) + X - 1 - x) + (1 - first) * (
        x * (Z - 1) + (1 - odd) * (z - 1) + odd * (Z - 1 - z)
    )

    def dev(offset, core):
        kk = lax.rem(k + offset + R, R)
        top = lax.div(kk, X * (Z - 1))
        xs = lax.div(kk, Z - 1)
        t = lax.rem(kk, Z - 1)
        o = lax.rem(xs, 2)
        zs = 1 + (1 - o) * t + o * (Z - 2 - t)
        xr = top * (X - 1 - (kk - X * (Z - 1))) + (1 - top) * xs
        zr = (1 - top) * zs
        return (zr * X + xr) * 2 + core

    nxt, prv = (g, dev(1, c)), (g, dev(-1, c))
    sib, oth = (g, me + 1 - 2 * c), (og, me)
    sc = 1 - c

    def pieces():
        step = kinv.shape[0] // PIECES
        for i in range(PIECES):
            rows = pl.ds(i * step, step)
            yield pltpu.make_async_copy(kinv_hbm.at[rows], kinv.at[rows], load_sem.at[2 + i])
        step = docs.shape[0] // PIECES
        for i in range(PIECES):
            rows = pl.ds(i * step, step)
            yield pltpu.make_async_copy(docs_hbm.at[rows], docs.at[rows], load_sem.at[2 + PIECES + i])

    columns = pl.ds(pl.multiple_of(g * width, width), width)
    own_q = [
        pltpu.make_async_copy(q_hbm.at[pl.ds(u * half, half), columns], qbuf.at[me, u], load_sem.at[u])
        for u in range(2)
    ]
    loads = list(pieces())
    for copy in own_q + loads:
        copy.start()

    barrier = pltpu.get_barrier_semaphore()
    for to in (nxt, prv, sib, oth):
        pl.semaphore_signal(barrier, inc=1, device_id=to, device_id_type=MESH)
    pl.semaphore_wait(barrier, 4)

    def rc(ref, ssem, rsem, to):
        return pltpu.make_async_remote_copy(
            src_ref=ref, dst_ref=ref, send_sem=ssem, recv_sem=rsem, device_id=to, device_id_type=MESH
        )

    def q_copy(b, u, ssem, to):
        return rc(qbuf.at[b, u], ssem, q_recv.at[b, u], to)

    def q_wait(b, u):
        q_copy(b, u, q_sib.at[b, u], sib).wait_recv()

    def q_cw(h, u):
        return q_copy(dev(-h, c), u, q_ring.at[0, h, u], nxt)

    def q_ccw(h, u):
        return q_copy(dev(h, c), u, q_ring.at[1, h, u], prv)

    def q_relay(b, u):
        return q_copy(b, u, q_sib.at[b, u], sib)

    def q_dot(b):
        rows = pl.ds(pl.multiple_of(b * depth, depth), depth)
        return lax.dot_general(
            qbuf[b].reshape(depth, width), kinv[rows, :], (((0,), (0,)), ((), ())),
            preferred_element_type=jnp.float32,
        )

    def q_add(b):
        acct[...] += q_dot(b)

    own_q[0].wait()
    own_q[1].wait()
    q_cw(0, 0).start()
    q_ccw(0, 1).start()
    q_cw(0, 1).start()
    q_ccw(0, 0).start()
    q_relay(me, 0).start()
    q_relay(me, 1).start()
    for copy in loads[:PIECES]:
        copy.wait()
    acct[...] = q_dot(me)

    def q_step(h, carry):
        left, right = dev(-h, c), dev(h, c)
        q_wait(left, 0)
        q_cw(h, 0).start()
        q_relay(left, 0).start()
        q_wait(right, 1)
        q_ccw(h, 1).start()
        q_relay(right, 1).start()
        sl, sr = dev(1 - h, sc), dev(h - 1, sc)
        q_wait(sl, 0)
        q_wait(sl, 1)
        q_add(sl)

        @pl.when(h > 1)
        def _():
            q_wait(sr, 0)
            q_wait(sr, 1)
            q_add(sr)

        q_wait(left, 1)

        @pl.when(h < H - 1)
        def _():
            q_cw(h, 1).start()

        q_relay(left, 1).start()
        q_wait(right, 0)

        @pl.when(h < H - 1)
        def _():
            q_ccw(h, 0).start()

        q_relay(right, 0).start()
        q_add(left)
        q_add(right)
        return carry

    lax.fori_loop(1, H, q_step, 0)
    far, sfar = dev(H, c), dev(H, sc)
    for b in (dev(1 - H, sc), dev(H - 1, sc)):
        q_wait(b, 0)
        q_wait(b, 1)
        q_add(b)
    q_wait(far, 0)
    q_relay(far, 0).start()
    q_wait(far, 1)
    q_relay(far, 1).start()
    q_add(far)
    q_wait(sfar, 0)
    q_wait(sfar, 1)
    q_add(sfar)
    pbuf[g, me] = jnp.transpose(acct[...]).astype(pbuf.dtype).reshape(2, half, width)

    def p_copy(hf, b, u, ssem, to):
        return rc(pbuf.at[hf, b, u], ssem, p_recv.at[hf, b, u], to)

    def p_wait(hf, b, u):
        p_copy(hf, b, u, p_sib.at[hf, b, u], sib).wait_recv()

    kinds = ((g, 0), (g, 1), (og, 1))

    def p_cw(h, t):
        hf, u = kinds[t]
        return p_copy(hf, dev(-h, c), u, p_ring.at[0, h, t], nxt)

    def p_ccw(h, t):
        hf, u = kinds[t]
        return p_copy(hf, dev(h, c), u, p_ring.at[1, h, t], prv)

    def p_relay(hf, b, u):
        return p_copy(hf, b, u, p_sib.at[hf, b, u], sib)

    def p_cross(b, u):
        return p_copy(g, b, u, p_y.at[b, u], oth)

    def p_dot(b):
        cols = pl.ds(pl.multiple_of(b * depth, depth), depth)
        block = jnp.concatenate(
            [pbuf[0, b].reshape(depth, width), pbuf[1, b].reshape(depth, width)], axis=1
        )
        return jnp.dot(docs[:, cols], block, preferred_element_type=jnp.float32)

    def p_add(b):
        out_ref[...] += p_dot(b)

    def p_wait_all(b):
        for hf in range(2):
            for u in range(2):
                p_wait(hf, b, u)

    p_cross(me, 1).start()
    p_cw(0, 0).start()
    p_ccw(0, 1).start()
    p_cw(0, 1).start()
    p_ccw(0, 0).start()
    p_cross(me, 0).start()
    p_relay(g, me, 0).start()
    p_relay(g, me, 1).start()
    out_ref[...] = jnp.zeros_like(out_ref)
    for copy in loads[PIECES:]:
        copy.wait()
    p_wait(og, me, 1)
    p_cw(0, 2).start()
    p_ccw(0, 2).start()
    p_relay(og, me, 1).start()
    p_wait(og, me, 0)
    p_relay(og, me, 0).start()
    p_add(me)

    def p_step(h, carry):
        left, right = dev(-h, c), dev(h, c)
        lb, rb = dev(1 - h, c), dev(h - 1, c)

        p_wait(g, left, 0)
        p_cw(h, 0).start()
        p_cross(left, 0).start()
        p_relay(g, left, 0).start()
        p_wait(g, right, 1)
        p_ccw(h, 1).start()
        p_relay(g, right, 1).start()

        @pl.when(h > 1)
        def _():
            p_wait(og, lb, 0)
            p_relay(og, lb, 0).start()
            p_wait(og, rb, 0)
            p_relay(og, rb, 0).start()
            p_add(lb)

        p_wait(g, left, 1)

        @pl.when(h < H - 1)
        def _():
            p_cw(h, 1).start()

        p_relay(g, left, 1).start()
        p_wait(g, right, 0)

        @pl.when(h < H - 1)
        def _():
            p_ccw(h, 0).start()

        p_cross(right, 0).start()
        p_relay(g, right, 0).start()

        @pl.when(h > 1)
        def _():
            p_add(rb)

        p_wait(og, left, 1)

        @pl.when((h < H - 1) | (c == 0))
        def _():
            p_cw(h, 2).start()

        p_relay(og, left, 1).start()
        p_wait(og, right, 1)

        @pl.when((h < H - 1) | (c == 1))
        def _():
            p_ccw(h, 2).start()

        p_relay(og, right, 1).start()
        sl, sr = dev(1 - h, sc), dev(h - 1, sc)
        p_wait_all(sl)
        p_add(sl)

        @pl.when(h > 1)
        def _():
            p_wait_all(sr)
            p_add(sr)

        return carry

    lax.fori_loop(1, H, p_step, 0)
    lb, rb = dev(1 - H, c), dev(H - 1, c)
    p_wait(og, lb, 0)
    p_relay(og, lb, 0).start()
    p_wait(og, rb, 0)
    p_relay(og, rb, 0).start()
    p_add(lb)
    p_wait(g, far, 0)
    p_cross(far, 0).start()
    p_relay(g, far, 0).start()
    p_wait(g, far, 1)
    p_relay(g, far, 1).start()
    p_add(rb)
    p_wait(og, far, 1)
    p_relay(og, far, 1).start()
    for b in (dev(1 - H, sc), dev(H - 1, sc)):
        p_wait_all(b)
        p_add(b)
    p_wait(og, far, 0)
    p_relay(og, far, 0).start()
    p_add(far)
    p_wait_all(sfar)
    p_add(sfar)

    def sent(h, carry):
        for b in (dev(-h, c), dev(h, c)):
            q_relay(b, 0).wait_send()
            q_relay(b, 1).wait_send()
            for hf in range(2):
                for u in range(2):
                    p_relay(hf, b, u).wait_send()
            p_cross(b, 0).wait_send()
        return carry

    lax.fori_loop(1, H, sent, 0)
    for b in (me, far):
        q_relay(b, 0).wait_send()
        q_relay(b, 1).wait_send()
        for hf in range(2):
            for u in range(2):
                p_relay(hf, b, u).wait_send()
        p_cross(b, 0).wait_send()
    p_cross(me, 1).wait_send()

    def ring_sent(h, carry):
        for u in range(2):
            q_cw(h, u).wait_send()
            q_ccw(h, u).wait_send()
        for t in range(3):
            p_cw(h, t).wait_send()
            p_ccw(h, t).wait_send()
        return carry

    lax.fori_loop(0, H - 1, ring_sent, 0)
    q_cw(H - 1, 0).wait_send()
    q_ccw(H - 1, 1).wait_send()
    p_cw(H - 1, 0).wait_send()
    p_ccw(H - 1, 1).wait_send()

    @pl.when(c == 0)
    def _():
        p_cw(H - 1, 2).wait_send()

    @pl.when(c == 1)
    def _():
        p_ccw(H - 1, 2).wait_send()


def ringed(n, X, documents, kernel_inverse, queries):
    rows, features = documents.shape
    depth, M = queries.shape
    half, width = depth // 2, M // 2
    H = n // 4
    dma = pltpu.SemaphoreType.DMA
    return pl.pallas_call(
        functools.partial(kernel, n, X),
        out_shape=jax.ShapeDtypeStruct((rows, M), jnp.float32),
        in_specs=[pl.BlockSpec(memory_space=pl.ANY)] * 3,
        out_specs=pl.BlockSpec(memory_space=pltpu.VMEM),
        scratch_shapes=[
            pltpu.VMEM((rows, features), jnp.bfloat16),
            pltpu.VMEM((features, depth), jnp.bfloat16),
            pltpu.VMEM((n, 2, half, width), jnp.bfloat16),
            pltpu.VMEM((2, n, 2, half, width), jnp.bfloat16),
            pltpu.VMEM((width, depth), jnp.float32),
            dma((2 + 2 * PIECES,)),
            dma((n, 2)),
            dma((2, H, 2)),
            dma((n, 2)),
            dma((2, n, 2)),
            dma((2, H, 3)),
            dma((2, n, 2)),
            dma((n, 2)),
        ],
        compiler_params=pltpu.CompilerParams(collective_id=0, has_side_effects=True),
        name="trak_ring",
    )(documents, kernel_inverse, queries)


def solution(mesh):
    groups, n = mesh.shape["groups"], mesh.shape["rows"]
    chips = n // 2
    X = 2 ** (int(math.log2(max(chips // 2, 1))) // 2)

    def local(documents, kernel_inverse, queries):
        depth, M = queries.shape
        fits = groups == 2 and n % 8 == 0 and depth % 256 == 0 and M % 256 == 0 and X % 2 == 0
        if not fits:
            return plain(documents, kernel_inverse, queries)
        return ringed(n, X, documents, kernel_inverse, queries)

    placed = (P(("groups", "rows"), None), P(None, "rows"), P("rows", None))
    return jax.shard_map(
        local, mesh=mesh, in_specs=placed, out_specs=P(("groups", "rows"), None), check_vma=False
    )
```

```python
import functools
import math

import jax
import jax.numpy as jnp
from jax import lax
from jax.experimental import pallas as pl
from jax.experimental.pallas import tpu as pltpu
from jax.sharding import PartitionSpec as P

MESH = pl.DeviceIdType.MESH
PIECES = 4
CUTS = 4


def plain(documents, kernel_inverse, queries):
    whole_queries = lax.all_gather(queries, "rows", axis=0, tiled=True)
    own_rows = lax.dot_general(
        kernel_inverse, whole_queries, (((0,), (0,)), ((), ())), preferred_element_type=jnp.float32
    ).astype(jnp.bfloat16)
    return jnp.dot(
        documents,
        lax.all_gather(own_rows, "rows", axis=0, tiled=True),
        preferred_element_type=jnp.float32,
    )


def kernel(
    n, X, docs_hbm, kinv_hbm, q_hbm, out_hbm,
    docs, kinv, qbuf, pbuf, acct, out_ref,
    load_sem, q_recv, q_ring, q_sib, p_recv, p_ring, p_sib, p_y,
):
    g, me = lax.axis_index("groups"), lax.axis_index("rows")
    og = 1 - g
    R = n // 2
    Z = R // X
    H = R // 2
    U, sub, width = qbuf.shape[1:]
    depth = U * sub
    low, high = tuple(range(U // 2)), tuple(range(U // 2, U))
    c = lax.rem(me, 2)
    chip = lax.div(me, 2)
    z, x = lax.div(chip, X), lax.rem(chip, X)
    first = lax.div(Z - z, Z)
    odd = lax.rem(x, 2)
    k = first * (X * (Z - 1) + X - 1 - x) + (1 - first) * (
        x * (Z - 1) + (1 - odd) * (z - 1) + odd * (Z - 1 - z)
    )

    def dev(offset, core):
        kk = lax.rem(k + offset + R, R)
        top = lax.div(kk, X * (Z - 1))
        xs = lax.div(kk, Z - 1)
        t = lax.rem(kk, Z - 1)
        o = lax.rem(xs, 2)
        zs = 1 + (1 - o) * t + o * (Z - 2 - t)
        xr = top * (X - 1 - (kk - X * (Z - 1))) + (1 - top) * xs
        zr = (1 - top) * zs
        return (zr * X + xr) * 2 + core

    nxt, prv = (g, dev(1, c)), (g, dev(-1, c))
    sib, oth = (g, me + 1 - 2 * c), (og, me)
    sc = 1 - c

    def pieces():
        step = kinv.shape[0] // PIECES
        for i in range(PIECES):
            rows = pl.ds(i * step, step)
            yield pltpu.make_async_copy(kinv_hbm.at[rows], kinv.at[rows], load_sem.at[U + i])
        step = docs.shape[0] // PIECES
        for i in range(PIECES):
            rows = pl.ds(i * step, step)
            yield pltpu.make_async_copy(docs_hbm.at[rows], docs.at[rows], load_sem.at[U + PIECES + i])

    columns = pl.ds(pl.multiple_of(g * width, width), width)
    own_q = [
        pltpu.make_async_copy(q_hbm.at[pl.ds(u * sub, sub), columns], qbuf.at[me, u], load_sem.at[u])
        for u in range(U)
    ]
    loads = list(pieces())
    for copy in own_q + loads:
        copy.start()

    barrier = pltpu.get_barrier_semaphore()
    for to in (nxt, prv, sib, oth):
        pl.semaphore_signal(barrier, inc=1, device_id=to, device_id_type=MESH)
    pl.semaphore_wait(barrier, 4)

    def rc(ref, ssem, rsem, to):
        return pltpu.make_async_remote_copy(
            src_ref=ref, dst_ref=ref, send_sem=ssem, recv_sem=rsem, device_id=to, device_id_type=MESH
        )

    q_orders = (low + high, high + low)

    def q_copy(b, u, ssem, to):
        return rc(qbuf.at[b, u], ssem, q_recv.at[b, u], to)

    def q_wait(b, u):
        q_copy(b, u, q_sib.at[b, u], sib).wait_recv()

    def q_hop(way, h, u):
        b = dev(h if way else -h, c)
        return q_copy(b, u, q_ring.at[way, h, u], prv if way else nxt)

    def q_relay(b, u):
        return q_copy(b, u, q_sib.at[b, u], sib)

    def q_dot(b):
        rows = pl.ds(pl.multiple_of(b * depth, depth), depth)
        return lax.dot_general(
            qbuf[b].reshape(depth, width), kinv[rows, :], (((0,), (0,)), ((), ())),
            preferred_element_type=jnp.float32,
        )

    def q_add(b):
        acct[...] += q_dot(b)

    def q_add_sib(b):
        for u in range(U):
            q_wait(b, u)
        q_add(b)

    for copy in own_q:
        copy.wait()
    for i in range(U):
        for way in range(2):
            q_hop(way, 0, q_orders[way][i]).start()
    for u in range(U):
        q_relay(me, u).start()
    for copy in loads[:PIECES]:
        copy.wait()
    acct[...] = q_dot(me)

    def q_step(h, carry):
        sides = (dev(-h, c), dev(h, c))
        for i in range(U):
            for way in range(2):
                u = q_orders[way][i]
                q_wait(sides[way], u)
                if i < U // 2:
                    q_hop(way, h, u).start()
                else:
                    @pl.when(h < H - 1)
                    def _():
                        q_hop(way, h, u).start()
                q_relay(sides[way], u).start()
            if i == 0:
                q_add_sib(dev(1 - h, sc))
            if i == 1:
                @pl.when(h > 1)
                def _():
                    q_add_sib(dev(h - 1, sc))
        for b in sides:
            q_add(b)
        return carry

    lax.fori_loop(1, H, q_step, 0)
    far, sfar = dev(H, c), dev(H, sc)
    ends = ((1 - H), (H - 1))
    for i in range(U // 2):
        for way in range(2):
            u = q_orders[way][i]
            q_wait(far, u)
            q_relay(far, u).start()
        q_add_sib(dev(ends[i % 2], sc)) if i < 2 else None
    q_add(far)
    q_add_sib(sfar)
    pbuf[g, me] = jnp.transpose(acct[...]).astype(pbuf.dtype).reshape(U, sub, width)

    mine = tuple((0, u) for u in range(U))
    orders = (
        tuple((0, u) for u in low + high) + tuple((1, u) for u in high),
        tuple((0, u) for u in high + low) + tuple((1, u) for u in high[::-1]),
    )
    T = len(orders[0])
    mid = len(high) // 2
    lasts = (
        tuple((0, u) for u in low) + tuple((1, u) for u in high[:mid]),
        tuple((0, u) for u in high) + tuple((1, u) for u in high[mid:]),
    )
    slot = {kind: t for t, kind in enumerate(orders[0])}
    halves = (g, og)

    def p_copy(kind, b, ssem, to):
        hf, u = halves[kind[0]], kind[1]
        return rc(pbuf.at[hf, b, u], ssem, p_recv.at[hf, b, u], to)

    def p_relay(kind, b):
        return p_copy(kind, b, p_sib.at[halves[kind[0]], b, kind[1]], sib)

    def p_wait(kind, b):
        p_relay(kind, b).wait_recv()

    def p_hop(way, h, kind):
        b = dev(h if way else -h, c)
        return p_copy(kind, b, p_ring.at[way, h, slot[kind]], prv if way else nxt)

    def p_cross(b, u):
        return p_copy((0, u), b, p_y.at[b, u], oth)

    def p_add(b):
        cols = pl.ds(pl.multiple_of(b * depth, depth), depth)
        block = jnp.concatenate(
            [pbuf[0, b].reshape(depth, width), pbuf[1, b].reshape(depth, width)], axis=1
        )
        out_ref[...] += jnp.dot(docs[:, cols], block, preferred_element_type=jnp.float32)

    def p_add_high(b):
        part = depth // 2
        cols = pl.ds(pl.multiple_of(b * depth + part, part), part)
        block = jnp.concatenate(
            [pbuf[i, b, U // 2 :].reshape(part, width) for i in range(2)], axis=1
        )
        out_ref[...] += jnp.dot(docs[:, cols], block, preferred_element_type=jnp.float32)

    def p_add_low(b, i):
        part = depth // 2
        hf = halves[i]
        cols = pl.ds(pl.multiple_of(b * depth, part), part)
        block = pbuf[hf, b, : U // 2].reshape(part, width)
        into = pl.ds(pl.multiple_of(hf * width, width), width)
        out_ref[:, into] += jnp.dot(docs[:, cols], block, preferred_element_type=jnp.float32)

    def p_cross_in(b):
        for u in low:
            p_wait((1, u), b)
            p_relay((1, u), b).start()

    def p_add_sib(b):
        for i in range(2):
            for u in range(U):
                p_wait((i, u), b)
        p_add(b)

    for u in high:
        p_cross(me, u).start()
    for i in range(U):
        for way in range(2):
            p_hop(way, 0, orders[way][i]).start()
    for u in low:
        p_cross(me, u).start()
    for kind in mine:
        p_relay(kind, me).start()
    out_ref[...] = jnp.zeros_like(out_ref)
    for copy in loads[PIECES:]:
        copy.wait()
    for u in high:
        p_wait((1, u), me)
    for i in range(U, T):
        for way in range(2):
            p_hop(way, 0, orders[way][i]).start()
    for u in high:
        p_relay((1, u), me).start()
    p_cross_in(me)
    p_add(me)

    def p_step(h, carry):
        sides = (dev(-h, c), dev(h, c))
        before = (dev(1 - h, c), dev(h - 1, c))
        for i in range(T):
            for way in range(2):
                kind = orders[way][i]
                p_wait(kind, sides[way])
                if kind in lasts[way]:
                    p_hop(way, h, kind).start()
                else:
                    @pl.when(h < H - 1)
                    def _():
                        p_hop(way, h, kind).start()
                if kind[0] == 0 and kind[1] in low:
                    p_cross(sides[way], kind[1]).start()
                p_relay(kind, sides[way]).start()
            for way, at in ((0, U // 2 - 1), (1, U - 1)):
                if i == at:
                    @pl.when(h > 1)
                    def _():
                        p_cross_in(before[way])
                        p_add(before[way])
        p_add_sib(dev(1 - h, sc))

        @pl.when(h > 1)
        def _():
            p_add_sib(dev(h - 1, sc))

        return carry

    lax.fori_loop(1, H, p_step, 0)
    for i in range(len(lasts[0])):
        for way in range(2):
            kind = lasts[way][i]
            p_wait(kind, far)
            if kind[0] == 0 and kind[1] in low:
                p_cross(far, kind[1]).start()
            p_relay(kind, far).start()
        if i < 2:
            b = dev(ends[i], c)
            p_cross_in(b)
            p_add(b)
    for e in ends:
        p_add_sib(dev(e, sc))
    p_add_high(far)
    p_add_low(far, 0)
    for i in range(2):
        for u in high:
            p_wait((i, u), sfar)
    p_add_high(sfar)
    for u in low:
        p_wait((0, u), sfar)
    p_add_low(sfar, 0)
    p_cross_in(far)
    p_add_low(far, 1)
    for u in low:
        p_wait((1, u), sfar)
    p_add_low(sfar, 1)
    result = pltpu.make_async_copy(out_ref, out_hbm, load_sem.at[0])
    result.start()

    def sent_block(b):
        for u in range(U):
            q_relay(b, u).wait_send()
            for i in range(2):
                p_relay((i, u), b).wait_send()
        for u in low:
            p_cross(b, u).wait_send()

    def sent(h, carry):
        for b in (dev(-h, c), dev(h, c)):
            sent_block(b)
        for way in range(2):
            for u in range(U):
                q_hop(way, h - 1, u).wait_send()
            for kind in orders[way]:
                p_hop(way, h - 1, kind).wait_send()
        return carry

    lax.fori_loop(1, H, sent, 0)
    for b in (me, far):
        sent_block(b)
    for u in high:
        p_cross(me, u).wait_send()
    for way in range(2):
        for u in q_orders[way][: U // 2]:
            q_hop(way, H - 1, u).wait_send()
        for kind in lasts[way]:
            p_hop(way, H - 1, kind).wait_send()
    result.wait()


def ringed(n, X, documents, kernel_inverse, queries):
    rows, features = documents.shape
    depth, M = queries.shape
    U, width = CUTS, M // 2
    sub = depth // U
    H = n // 4
    dma = pltpu.SemaphoreType.DMA
    return pl.pallas_call(
        functools.partial(kernel, n, X),
        out_shape=jax.ShapeDtypeStruct((rows, M), jnp.float32),
        in_specs=[pl.BlockSpec(memory_space=pl.ANY)] * 3,
        out_specs=pl.BlockSpec(memory_space=pl.ANY),
        scratch_shapes=[
            pltpu.VMEM((rows, features), jnp.bfloat16),
            pltpu.VMEM((features, depth), jnp.bfloat16),
            pltpu.VMEM((n, U, sub, width), jnp.bfloat16),
            pltpu.VMEM((2, n, U, sub, width), jnp.bfloat16),
            pltpu.VMEM((width, depth), jnp.float32),
            pltpu.VMEM((rows, M), jnp.float32),
            dma((U + 2 * PIECES,)),
            dma((n, U)),
            dma((2, H, U)),
            dma((n, U)),
            dma((2, n, U)),
            dma((2, H, U + U // 2)),
            dma((2, n, U)),
            dma((n, U)),
        ],
        compiler_params=pltpu.CompilerParams(collective_id=0, has_side_effects=True),
        name="trak_ring",
    )(documents, kernel_inverse, queries)


def solution(mesh):
    groups, n = mesh.shape["groups"], mesh.shape["rows"]
    chips = n // 2
    X = 2 ** (int(math.log2(max(chips // 2, 1))) // 2)

    def local(documents, kernel_inverse, queries):
        depth, M = queries.shape
        fits = groups == 2 and n % 8 == 0 and depth % (32 * CUTS) == 0 and depth % 256 == 0 and M % 256 == 0 and X % 2 == 0
        if not fits:
            return plain(documents, kernel_inverse, queries)
        return ringed(n, X, documents, kernel_inverse, queries)

    placed = (P(("groups", "rows"), None), P(None, "rows"), P("rows", None))
    return jax.shard_map(
        local, mesh=mesh, in_specs=placed, out_specs=P(("groups", "rows"), None), check_vma=False
    )
```

```python
import functools
import math

import jax
import jax.numpy as jnp
from jax import lax
from jax.experimental import pallas as pl
from jax.experimental.pallas import tpu as pltpu
from jax.sharding import PartitionSpec as P

MESH = pl.DeviceIdType.MESH
PIECES = 4
CUTS = 4


def plain(documents, kernel_inverse, queries):
    whole_queries = lax.all_gather(queries, "rows", axis=0, tiled=True)
    own_rows = lax.dot_general(
        kernel_inverse, whole_queries, (((0,), (0,)), ((), ())), preferred_element_type=jnp.float32
    ).astype(jnp.bfloat16)
    return jnp.dot(
        documents,
        lax.all_gather(own_rows, "rows", axis=0, tiled=True),
        preferred_element_type=jnp.float32,
    )


def kernel(
    n, X, docs_hbm, kinv_hbm, q_hbm, out_ref,
    docs, kinv, qbuf, pbuf, acct,
    load_sem, q_recv, q_ring, q_sib, p_recv, p_ring, p_sib, p_y,
):
    g, me = lax.axis_index("groups"), lax.axis_index("rows")
    og = 1 - g
    R = n // 2
    Z = R // X
    H = R // 2
    U, sub, width = qbuf.shape[1:]
    depth = U * sub
    low, high = tuple(range(U // 2)), tuple(range(U // 2, U))
    c = lax.rem(me, 2)
    chip = lax.div(me, 2)
    z, x = lax.div(chip, X), lax.rem(chip, X)
    first = lax.div(Z - z, Z)
    odd = lax.rem(x, 2)
    k = first * (X * (Z - 1) + X - 1 - x) + (1 - first) * (
        x * (Z - 1) + (1 - odd) * (z - 1) + odd * (Z - 1 - z)
    )

    def dev(offset, core):
        kk = lax.rem(k + offset + R, R)
        top = lax.div(kk, X * (Z - 1))
        xs = lax.div(kk, Z - 1)
        t = lax.rem(kk, Z - 1)
        o = lax.rem(xs, 2)
        zs = 1 + (1 - o) * t + o * (Z - 2 - t)
        xr = top * (X - 1 - (kk - X * (Z - 1))) + (1 - top) * xs
        zr = (1 - top) * zs
        return (zr * X + xr) * 2 + core

    nxt, prv = (g, dev(1, c)), (g, dev(-1, c))
    sib, oth = (g, me + 1 - 2 * c), (og, me)
    diag = (og, me + 1 - 2 * c)
    sc = 1 - c

    def pieces():
        step = kinv.shape[0] // PIECES
        for i in range(PIECES):
            rows = pl.ds(i * step, step)
            yield pltpu.make_async_copy(kinv_hbm.at[rows], kinv.at[rows], load_sem.at[U + i])
        step = docs.shape[0] // PIECES
        for i in range(PIECES):
            rows = pl.ds(i * step, step)
            yield pltpu.make_async_copy(docs_hbm.at[rows], docs.at[rows], load_sem.at[U + PIECES + i])

    columns = pl.ds(pl.multiple_of(g * width, width), width)
    own_q = [
        pltpu.make_async_copy(q_hbm.at[pl.ds(u * sub, sub), columns], qbuf.at[me, u], load_sem.at[u])
        for u in range(U)
    ]
    loads = list(pieces())
    for copy in own_q + loads:
        copy.start()

    barrier = pltpu.get_barrier_semaphore()
    for to in (nxt, prv, sib, oth, diag):
        pl.semaphore_signal(barrier, inc=1, device_id=to, device_id_type=MESH)
    pl.semaphore_wait(barrier, 5)

    def rc(ref, ssem, rsem, to):
        return pltpu.make_async_remote_copy(
            src_ref=ref, dst_ref=ref, send_sem=ssem, recv_sem=rsem, device_id=to, device_id_type=MESH
        )

    q_orders = (low + high, high + low)

    def q_copy(b, u, ssem, to):
        return rc(qbuf.at[b, u], ssem, q_recv.at[b, u], to)

    def q_wait(b, u):
        q_copy(b, u, q_sib.at[b, u], sib).wait_recv()

    def q_hop(way, h, u):
        b = dev(h if way else -h, c)
        return q_copy(b, u, q_ring.at[way, h, u], prv if way else nxt)

    def q_relay(b, u):
        return q_copy(b, u, q_sib.at[b, u], sib)

    def q_dot(b):
        rows = pl.ds(pl.multiple_of(b * depth, depth), depth)
        return lax.dot_general(
            qbuf[b].reshape(depth, width), kinv[rows, :], (((0,), (0,)), ((), ())),
            preferred_element_type=jnp.float32,
        )

    def q_add(b):
        acct[...] += q_dot(b)

    def q_add_sib(b):
        for u in range(U):
            q_wait(b, u)
        q_add(b)

    for copy in own_q:
        copy.wait()
    for i in range(U):
        for way in range(2):
            q_hop(way, 0, q_orders[way][i]).start()
    for u in range(U):
        q_relay(me, u).start()
    for copy in loads[:PIECES]:
        copy.wait()
    acct[...] = q_dot(me)

    def q_step(h, carry):
        sides = (dev(-h, c), dev(h, c))
        for i in range(U):
            for way in range(2):
                u = q_orders[way][i]
                q_wait(sides[way], u)
                if i < U // 2:
                    q_hop(way, h, u).start()
                else:
                    @pl.when(h < H - 1)
                    def _():
                        q_hop(way, h, u).start()
                q_relay(sides[way], u).start()
            if i == 0:
                q_add_sib(dev(1 - h, sc))
            if i == 1:
                @pl.when(h > 1)
                def _():
                    q_add_sib(dev(h - 1, sc))
        for b in sides:
            q_add(b)
        return carry

    lax.fori_loop(1, H, q_step, 0)
    far, sfar = dev(H, c), dev(H, sc)
    ends = ((1 - H), (H - 1))
    for i in range(U // 2):
        for way in range(2):
            u = q_orders[way][i]
            q_wait(far, u)
            q_relay(far, u).start()
        q_add_sib(dev(ends[i % 2], sc)) if i < 2 else None
    q_add(far)
    q_add_sib(sfar)
    pbuf[g, me] = jnp.transpose(acct[...]).astype(pbuf.dtype).reshape(U, sub, width)

    mine = tuple((0, u) for u in range(U))
    orders = (
        tuple((0, u) for u in low + high) + tuple((1, u) for u in high),
        tuple((0, u) for u in high + low) + tuple((1, u) for u in high[::-1]),
    )
    T = len(orders[0])
    mid = len(high) // 2
    lasts = (
        tuple((0, u) for u in low) + tuple((1, u) for u in high[:mid]),
        tuple((0, u) for u in high) + tuple((1, u) for u in high[mid:]),
    )
    slot = {kind: t for t, kind in enumerate(orders[0])}
    halves = (g, og)

    def p_copy(kind, b, ssem, to):
        hf, u = halves[kind[0]], kind[1]
        return rc(pbuf.at[hf, b, u], ssem, p_recv.at[hf, b, u], to)

    def p_relay(kind, b):
        return p_copy(kind, b, p_sib.at[halves[kind[0]], b, kind[1]], sib)

    def p_wait(kind, b):
        p_relay(kind, b).wait_recv()

    def p_hop(way, h, kind):
        b = dev(h if way else -h, c)
        return p_copy(kind, b, p_ring.at[way, h, slot[kind]], prv if way else nxt)

    def p_cross(b, u):
        return p_copy((0, u), b, p_y.at[b, u], oth)

    def p_diag(b, u):
        return p_copy((0, u), b, p_sib.at[og, b, u], diag)

    def p_add(b):
        cols = pl.ds(pl.multiple_of(b * depth, depth), depth)
        block = jnp.concatenate(
            [pbuf[0, b].reshape(depth, width), pbuf[1, b].reshape(depth, width)], axis=1
        )
        out_ref[...] += jnp.dot(docs[:, cols], block, preferred_element_type=jnp.float32)

    def p_add_high(b):
        part = depth // 2
        cols = pl.ds(pl.multiple_of(b * depth + part, part), part)
        block = jnp.concatenate(
            [pbuf[i, b, U // 2 :].reshape(part, width) for i in range(2)], axis=1
        )
        out_ref[...] += jnp.dot(docs[:, cols], block, preferred_element_type=jnp.float32)

    def p_add_low(b, i):
        part = depth // 2
        hf = halves[i]
        cols = pl.ds(pl.multiple_of(b * depth, part), part)
        block = pbuf[hf, b, : U // 2].reshape(part, width)
        into = pl.ds(pl.multiple_of(hf * width, width), width)
        out_ref[:, into] += jnp.dot(docs[:, cols], block, preferred_element_type=jnp.float32)

    def p_cross_in(b):
        for u in low:
            p_wait((1, u), b)
            p_relay((1, u), b).start()

    def p_add_sib(b):
        for i in range(2):
            for u in range(U):
                p_wait((i, u), b)
        p_add(b)

    for u in high:
        p_cross(me, u).start()
    for i in range(U):
        for way in range(2):
            p_hop(way, 0, orders[way][i]).start()
    for u in low:
        p_cross(me, u).start()
    for kind in mine:
        p_relay(kind, me).start()
    out_ref[...] = jnp.zeros_like(out_ref)
    for copy in loads[PIECES:]:
        copy.wait()
    for u in high:
        p_wait((1, u), me)
    for i in range(U, T):
        for way in range(2):
            p_hop(way, 0, orders[way][i]).start()
    for u in high:
        p_relay((1, u), me).start()
    p_cross_in(me)
    p_add(me)

    def p_step(h, carry):
        sides = (dev(-h, c), dev(h, c))
        before = (dev(1 - h, c), dev(h - 1, c))
        for i in range(T):
            for way in range(2):
                kind = orders[way][i]
                p_wait(kind, sides[way])
                if kind in lasts[way]:
                    p_hop(way, h, kind).start()
                else:
                    @pl.when(h < H - 1)
                    def _():
                        p_hop(way, h, kind).start()
                if kind[0] == 0 and kind[1] in low:
                    p_cross(sides[way], kind[1]).start()
                p_relay(kind, sides[way]).start()
            for way, at in ((0, U // 2 - 1), (1, U - 1)):
                if i == at:
                    @pl.when(h > 1)
                    def _():
                        p_cross_in(before[way])
                        p_add(before[way])
        p_add_sib(dev(1 - h, sc))

        @pl.when(h > 1)
        def _():
            p_add_sib(dev(h - 1, sc))

        return carry

    lax.fori_loop(1, H, p_step, 0)
    for i in range(len(lasts[0])):
        for way in range(2):
            kind = lasts[way][i]
            p_wait(kind, far)
            if kind[0] == 0 and kind[1] in low:
                p_cross(far, kind[1]).start()
                p_diag(far, kind[1]).start()
            p_relay(kind, far).start()
        if i < 2:
            b = dev(ends[i], c)
            p_cross_in(b)
            p_add(b)
    for e in ends:
        p_add_sib(dev(e, sc))
    p_add_high(far)
    p_add_low(far, 0)
    for i in range(2):
        for u in high:
            p_wait((i, u), sfar)
    p_add_high(sfar)
    for u in low:
        p_wait((0, u), sfar)
    p_add_low(sfar, 0)
    for u in low:
        p_wait((1, u), far)
    p_add_low(far, 1)
    for u in low:
        p_wait((1, u), sfar)
    p_add_low(sfar, 1)

    def sent_block(b):
        for u in range(U):
            q_relay(b, u).wait_send()
            for i in range(2):
                p_relay((i, u), b).wait_send()
        for u in low:
            p_cross(b, u).wait_send()

    def sent(h, carry):
        for b in (dev(-h, c), dev(h, c)):
            sent_block(b)
        for way in range(2):
            for u in range(U):
                q_hop(way, h - 1, u).wait_send()
            for kind in orders[way]:
                p_hop(way, h - 1, kind).wait_send()
        return carry

    lax.fori_loop(1, H, sent, 0)
    for b in (me, far):
        sent_block(b)
    for u in high:
        p_cross(me, u).wait_send()
    for way in range(2):
        for u in q_orders[way][: U // 2]:
            q_hop(way, H - 1, u).wait_send()
        for kind in lasts[way]:
            p_hop(way, H - 1, kind).wait_send()


def ringed(n, X, documents, kernel_inverse, queries):
    rows, features = documents.shape
    depth, M = queries.shape
    U, width = CUTS, M // 2
    sub = depth // U
    H = n // 4
    dma = pltpu.SemaphoreType.DMA
    return pl.pallas_call(
        functools.partial(kernel, n, X),
        out_shape=pltpu.VMEM((rows, M), jnp.float32),
        in_specs=[pl.BlockSpec(memory_space=pl.ANY)] * 3,
        out_specs=pl.BlockSpec(memory_space=pltpu.VMEM),
        scratch_shapes=[
            pltpu.VMEM((rows, features), jnp.bfloat16),
            pltpu.VMEM((features, depth), jnp.bfloat16),
            pltpu.VMEM((n, U, sub, width), jnp.bfloat16),
            pltpu.VMEM((2, n, U, sub, width), jnp.bfloat16),
            pltpu.VMEM((width, depth), jnp.float32),
            dma((U + 2 * PIECES,)),
            dma((n, U)),
            dma((2, H, U)),
            dma((n, U)),
            dma((2, n, U)),
            dma((2, H, U + U // 2)),
            dma((2, n, U)),
            dma((n, U)),
        ],
        compiler_params=pltpu.CompilerParams(collective_id=0, has_side_effects=True, vmem_limit_bytes=56 * 2**20),
        name="trak_ring",
    )(documents, kernel_inverse, queries)


def solution(mesh):
    groups, n = mesh.shape["groups"], mesh.shape["rows"]
    chips = n // 2
    X = 2 ** (int(math.log2(max(chips // 2, 1))) // 2)

    def local(documents, kernel_inverse, queries):
        depth, M = queries.shape
        fits = groups == 2 and n % 8 == 0 and depth % (32 * CUTS) == 0 and depth % 256 == 0 and M % 256 == 0 and X % 2 == 0
        if not fits:
            return plain(documents, kernel_inverse, queries)
        return ringed(n, X, documents, kernel_inverse, queries)

    placed = (P(("groups", "rows"), None), P(None, "rows"), P("rows", None))
    return jax.shard_map(
        local, mesh=mesh, in_specs=placed, out_specs=P(("groups", "rows"), None), check_vma=False
    )
```
